32 devices in a mesh: site: 16 (over z, y, x), sec: 2 (over core).
Axes of the slice: x: 2, y: 2, z: 4, core: 2. Of those that a mesh axis runs over, the one named last changes fastest.
Arguments:
- env_in: float32 [16, 16, 256, 256], P('site', 'sec'), may hold values from -6 to 6
- ket: bfloat16 [16, 4, 16, 256, 256], P('site', None, 'sec'), may hold values from -0.1875 to 0.1875
- bra: bfloat16 [16, 4, 16, 256, 256], P('site', None, 'sec'), may hold values from -0.375 to 0.375
- source: int32 [16, 4, 16], P('site'), may hold values from 0 to 15, each once within a row
Outputs:
- env_out: float32 [16, 16, 256, 256], P('site', 'sec')
The draws below stay inside these ranges and needn't reach their ends.
Inputs may be any that keep to these rules, and one draw needn't show every extreme that they name: For every site s and physical state p, source[s, p, :] is a permutation of the 16 sectors.
All inputs are finite; a program needn't handle non-finite values.
Results may differ from the reference program's by a relative error of at most 0.013.
Values may be sent and summed in bfloat16 or wider, within the bound.
A program may use at most 64 MiB of HBM per device.

```python
import jax
import jax.numpy as jnp
from jax import lax

B = 256
S = 16
P_SIZE = 4
ITERS = 4
SITES = 16


def steps_of(key, extent, split, smallest, high):
    def one(dim, blocks):
        steps = jax.random.uniform(jax.random.fold_in(jax.random.fold_in(key, 6), dim), (blocks,), jnp.float32, smallest / len(split), high / len(split))
        return jnp.repeat(jnp.exp(steps), extent[dim] // blocks).reshape((-1,) + (1,) * (len(extent) - dim - 1))

    level = one(*split[0])
    for cut in split[1:]:
        level = level * one(*cut)
    return level


def noise(stream_key, dims, width, bound, shards=(), dtype=jnp.bfloat16):
    level = steps_of(stream_key, dims, shards, -0.22, 0.18) if shards else 1.0
    result = jax.random.normal(stream_key, dims, jnp.float32) * width * level
    return jnp.minimum(jnp.maximum(result, -bound), bound).astype(dtype)


def setup_inputs(seed: int = 0) -> dict:
    seeds = jax.random.split(jax.random.key(seed), 5)
    return {
        "env_in": noise(seeds[0], (SITES, S, B, B), 1.0, 6.0, ((0, 16), (1, 2)), jnp.float32),
        "ket": noise(seeds[1], (SITES, P_SIZE, S, B, B), (B * P_SIZE) ** -0.5, 0.1875, ((0, 16), (2, 2))),
        "bra": noise(seeds[2], (SITES, P_SIZE, S, B, B), B ** -0.5, 0.375, ((0, 16), (2, 2))),
        "source": jax.vmap(lambda own: jax.random.permutation(own, S))(jax.random.split(seeds[3], SITES * P_SIZE)).reshape((SITES, P_SIZE, S)).astype(jnp.int32),
    }


def site_step(operands):
    low_site, ket_site, bra_site, source_site = operands
    picked = low_site[source_site.astype(jnp.int32)]
    half = jnp.einsum("pbij,pbjk->pbik", picked.astype(jnp.float32), ket_site.astype(jnp.float32)).astype(jnp.bfloat16)
    return jnp.einsum("pbji,pbjk->bik", bra_site.astype(jnp.float32), half.astype(jnp.float32))


def reference(env_in, ket, bra, source):
    current = env_in
    for step in range(ITERS):
        low = current.astype(jnp.bfloat16)
        following = lax.map(site_step, (low, ket, bra, source))
        current = jnp.roll(following, 1, axis=0)
    return current
```

```python
import functools

import jax
import jax.numpy as jnp
from jax import lax
from jax.experimental import pallas as pl
from jax.experimental.pallas import tpu as pltpu
from jax.sharding import PartitionSpec as P

ITERS = 4
MESH = pl.DeviceIdType.MESH


def kernel(
    sites, groups, source_ref, env_hbm, ket_hbm, bra_hbm, out_ref,
    env, ket, bra, bra_t, staged,
    env_sem, ket_sem, bra_sem, share_send, share_recv, hop_send, hop_recv, *low,
):
    site = lax.axis_index("site")
    sec = lax.axis_index("sec")
    states, own = ket.shape[0], ket.shape[1]
    first = sec * own
    after = lax.rem(site + 1, sites)
    before = lax.rem(site + sites - 1, sites)

    def sibling(k):
        return lax.rem(sec + k, groups)

    def load_env(b):
        return pltpu.make_async_copy(env_hbm.at[b], env.at[b], env_sem.at[b])

    def load_ket(b):
        return pltpu.make_async_copy(ket_hbm.at[:, b], ket.at[:, b], ket_sem.at[b])

    def load_bra(b):
        return pltpu.make_async_copy(bra_hbm.at[:, b], bra.at[:, b], bra_sem.at[b])

    def share(t, k, b):
        return pltpu.make_async_remote_copy(
            src_ref=low[t].at[first + b],
            dst_ref=low[t].at[first + b],
            send_sem=share_send.at[t, k - 1, b],
            recv_sem=share_recv.at[t, k - 1, b],
            device_id=(site, sibling(k)),
            device_id_type=MESH,
        )

    def shared(t, k, b):
        row = lax.rem(sec + groups - k, groups) * own + b
        return pltpu.make_async_remote_copy(
            src_ref=low[t].at[row],
            dst_ref=low[t].at[row],
            send_sem=share_send.at[t, k - 1, b],
            recv_sem=share_recv.at[t, k - 1, b],
            device_id=(site, sibling(k)),
            device_id_type=MESH,
        )

    def hop(t, b):
        return pltpu.make_async_remote_copy(
            src_ref=staged.at[t, b],
            dst_ref=low[t + 1].at[first + b] if t < ITERS - 1 else out_ref.at[b],
            send_sem=hop_send.at[t, b],
            recv_sem=hop_recv.at[t, b],
            device_id=(after, sec),
            device_id_type=MESH,
        )

    def each(body):
        def one(b, carry):
            body(b)
            return carry

        lax.fori_loop(0, own, one, 0)

    each(lambda b: load_env(b).start())
    each(lambda b: load_ket(b).start())
    each(lambda b: load_bra(b).start())

    barrier = pltpu.get_barrier_semaphore()
    for peer in [(after, sec), (before, sec)] + [(site, sibling(k)) for k in range(1, groups)]:
        pl.semaphore_signal(barrier, inc=1, device_id=peer, device_id_type=MESH)
    pl.semaphore_wait(barrier, groups + 1)

    def open_own(b):
        load_env(b).wait()
        low[0][first + b] = env[b].astype(jnp.bfloat16)
        for k in range(1, groups):
            share(0, k, b).start()

    each(open_own)

    def advance(t, b):
        total = None
        for p in range(states):
            if t == 0:
                bra_t[p, b] = bra[p, b].T
            picked = low[t][source_ref[p, first + b]]
            half = jnp.dot(picked, ket[p, b], preferred_element_type=jnp.float32).astype(jnp.bfloat16)
            term = jnp.dot(bra_t[p, b], half, preferred_element_type=jnp.float32)
            total = term if total is None else total + term
        staged[t, b] = total.astype(jnp.bfloat16)
        hop(t, b).start()

    for t in range(ITERS):
        if t > 0:

            def pass_on(b, t=t):
                hop(t - 1, b).wait_recv()
                for k in range(1, groups):
                    share(t, k, b).start()

            each(pass_on)

        def arrive(b, t=t):
            for k in range(1, groups):
                shared(t, k, b).wait_recv()

        each(arrive)

        def work(b, t=t):
            if t == 0:
                load_ket(b).wait()
                load_bra(b).wait()
            advance(t, b)

        each(work)

    def finish(b):
        for t in range(ITERS):
            hop(t, b).wait_send()
            for k in range(1, groups):
                share(t, k, b).wait_send()
        hop(ITERS - 1, b).wait_recv()

    each(finish)


def body(sites, groups, env_in, ket, bra, source):
    _, states, own, rows, cols = ket.shape
    whole = own * groups
    low = jnp.bfloat16
    arrived = pl.pallas_call(
        functools.partial(kernel, sites, groups),
        out_shape=jax.ShapeDtypeStruct((own, rows, cols), low),
        in_specs=[pl.BlockSpec(memory_space=pltpu.SMEM)] + [pl.BlockSpec(memory_space=pl.ANY)] * 3,
        out_specs=pl.BlockSpec(memory_space=pltpu.VMEM),
        scratch_shapes=[
            pltpu.VMEM((own, rows, cols), jnp.float32),
            pltpu.VMEM((states, own, rows, cols), low),
            pltpu.VMEM((states, own, rows, cols), low),
            pltpu.VMEM((states, own, rows, cols), low),
            pltpu.VMEM((ITERS, own, rows, cols), low),
            pltpu.SemaphoreType.DMA((own,)),
            pltpu.SemaphoreType.DMA((own,)),
            pltpu.SemaphoreType.DMA((own,)),
            pltpu.SemaphoreType.DMA((ITERS, groups - 1, own)),
            pltpu.SemaphoreType.DMA((ITERS, groups - 1, own)),
            pltpu.SemaphoreType.DMA((ITERS, own)),
            pltpu.SemaphoreType.DMA((ITERS, own)),
        ]
        + [pltpu.VMEM((whole, rows, cols), low)] * ITERS,
        compiler_params=pltpu.CompilerParams(collective_id=0, has_side_effects=True),
    )(source[0], env_in[0], ket[0], bra[0])
    return arrived.astype(jnp.float32)[None]


def solution(mesh):
    in_specs = (
        P("site", "sec", None, None),
        P("site", None, "sec", None, None),
        P("site", None, "sec", None, None),
        P("site", None, None),
    )
    out_specs = P("site", "sec", None, None)
    part = functools.partial(body, mesh.shape["site"], mesh.shape["sec"])
    return jax.shard_map(part, mesh=mesh, in_specs=in_specs, out_specs=out_specs, check_vma=False)
```

```python
import functools

import jax
import jax.numpy as jnp
from jax import lax
from jax.experimental import pallas as pl
from jax.experimental.pallas import tpu as pltpu
from jax.sharding import PartitionSpec as P

ITERS = 4
PIECES = 2
MESH = pl.DeviceIdType.MESH


def kernel(
    sites, groups, source_ref, env_hbm, ket_hbm, bra_hbm, out_ref,
    env, ket, bra, bra_t, halves, staged,
    env_sem, ket_sem, bra_sem, share_send, share_recv, hop_send, hop_recv, *low,
):
    site = lax.axis_index("site")
    sec = lax.axis_index("sec")
    states, own, rows = ket.shape[:3]
    first = sec * own
    after = lax.rem(site + 1, sites)
    before = lax.rem(site + sites - 1, sites)

    def sibling(k):
        return lax.rem(sec + k, groups)

    def load_env(b):
        return pltpu.make_async_copy(env_hbm.at[b], env.at[b], env_sem.at[b])

    def load_ket(b):
        return pltpu.make_async_copy(ket_hbm.at[:, b], ket.at[:, b], ket_sem.at[b])

    def load_bra(b):
        return pltpu.make_async_copy(bra_hbm.at[:, b], bra.at[:, b], bra_sem.at[b])

    def share(t, k, b):
        return pltpu.make_async_remote_copy(
            src_ref=low[t].at[first + b],
            dst_ref=low[t].at[first + b],
            send_sem=share_send.at[t, k - 1, b],
            recv_sem=share_recv.at[t, k - 1, b],
            device_id=(site, sibling(k)),
            device_id_type=MESH,
        )

    def shared(t, k, b):
        row = lax.rem(sec + groups - k, groups) * own + b
        return pltpu.make_async_remote_copy(
            src_ref=low[t].at[row],
            dst_ref=low[t].at[row],
            send_sem=share_send.at[t, k - 1, b],
            recv_sem=share_recv.at[t, k - 1, b],
            device_id=(site, sibling(k)),
            device_id_type=MESH,
        )

    def hop(t, b, q):
        part = pl.ds(q * rows // PIECES, rows // PIECES)
        return pltpu.make_async_remote_copy(
            src_ref=staged.at[t, b, part],
            dst_ref=low[t + 1].at[first + b, part] if t < ITERS - 1 else out_ref.at[b, part],
            send_sem=hop_send.at[t, b, q],
            recv_sem=hop_recv.at[t, b, q],
            device_id=(after, sec),
            device_id_type=MESH,
        )

    def each(body):
        def one(b, carry):
            body(b)
            return carry

        lax.fori_loop(0, own, one, 0)

    each(lambda b: load_env(b).start())
    each(lambda b: load_ket(b).start())
    each(lambda b: load_bra(b).start())

    barrier = pltpu.get_barrier_semaphore()
    for peer in [(after, sec), (before, sec)] + [(site, sibling(k)) for k in range(1, groups)]:
        pl.semaphore_signal(barrier, inc=1, device_id=peer, device_id_type=MESH)
    pl.semaphore_wait(barrier, groups + 1)

    def open_own(b):
        load_env(b).wait()
        low[0][first + b] = env[b].astype(jnp.bfloat16)
        for k in range(1, groups):
            share(0, k, b).start()

    each(open_own)

    def advance(t, b):
        for p in range(states):
            if t == 0:
                bra_t[b, :, p * rows : (p + 1) * rows] = bra[p, b].T
            picked = low[t][source_ref[p, first + b]]
            half = jnp.dot(picked, ket[p, b], preferred_element_type=jnp.float32)
            halves[p * rows : (p + 1) * rows] = half.astype(jnp.bfloat16)
        for q in range(PIECES):
            part = pl.ds(q * rows // PIECES, rows // PIECES)
            total = jnp.dot(bra_t[b, part], halves[...], preferred_element_type=jnp.float32)
            staged[t, b, part] = total.astype(jnp.bfloat16)
            hop(t, b, q).start()

    for t in range(ITERS):
        if t > 0:

            def pass_on(b, t=t):
                for q in range(PIECES):
                    hop(t - 1, b, q).wait_recv()
                for k in range(1, groups):
                    share(t, k, b).start()

            each(pass_on)

        def arrive(b, t=t):
            for k in range(1, groups):
                shared(t, k, b).wait_recv()

        each(arrive)

        def work(b, t=t):
            if t == 0:
                load_ket(b).wait()
                load_bra(b).wait()
            advance(t, b)

        each(work)

    def finish(b):
        for t in range(ITERS):
            for q in range(PIECES):
                hop(t, b, q).wait_send()
            for k in range(1, groups):
                share(t, k, b).wait_send()
        for q in range(PIECES):
            hop(ITERS - 1, b, q).wait_recv()

    each(finish)


def body(sites, groups, env_in, ket, bra, source):
    _, states, own, rows, cols = ket.shape
    whole = own * groups
    low = jnp.bfloat16
    arrived = pl.pallas_call(
        functools.partial(kernel, sites, groups),
        out_shape=jax.ShapeDtypeStruct((own, rows, cols), low),
        in_specs=[pl.BlockSpec(memory_space=pltpu.SMEM)] + [pl.BlockSpec(memory_space=pl.ANY)] * 3,
        out_specs=pl.BlockSpec(memory_space=pl.ANY),
        scratch_shapes=[
            pltpu.VMEM((own, rows, cols), jnp.float32),
            pltpu.VMEM((states, own, rows, cols), low),
            pltpu.VMEM((states, own, rows, cols), low),
            pltpu.VMEM((own, cols, states * rows), low),
            pltpu.VMEM((states * rows, cols), low),
            pltpu.VMEM((ITERS, own, rows, cols), low),
            pltpu.SemaphoreType.DMA((own,)),
            pltpu.SemaphoreType.DMA((own,)),
            pltpu.SemaphoreType.DMA((own,)),
            pltpu.SemaphoreType.DMA((ITERS, groups - 1, own)),
            pltpu.SemaphoreType.DMA((ITERS, groups - 1, own)),
            pltpu.SemaphoreType.DMA((ITERS, own, PIECES)),
            pltpu.SemaphoreType.DMA((ITERS, own, PIECES)),
        ]
        + [pltpu.VMEM((whole, rows, cols), low)] * ITERS,
        compiler_params=pltpu.CompilerParams(collective_id=0, has_side_effects=True),
    )(source[0], env_in[0], ket[0], bra[0])
    return arrived.astype(jnp.float32)[None]


def solution(mesh):
    in_specs = (
        P("site", "sec", None, None),
        P("site", None, "sec", None, None),
        P("site", None, "sec", None, None),
        P("site", None, None),
    )
    out_specs = P("site", "sec", None, None)
    part = functools.partial(body, mesh.shape["site"], mesh.shape["sec"])
    return jax.shard_map(part, mesh=mesh, in_specs=in_specs, out_specs=out_specs, check_vma=False)
```

```python
import functools

import jax
import jax.numpy as jnp
from jax import lax
from jax.experimental import pallas as pl
from jax.experimental.pallas import tpu as pltpu
from jax.sharding import PartitionSpec as P

ITERS = 4
PIECES = 2
MESH = pl.DeviceIdType.MESH


def kernel(
    sites, groups, source_ref, env_hbm, ket_hbm, bra_hbm, out_ref,
    env, ket, bra, bra_t, halves, staged,
    env_sem, ket_sem, bra_sem, share_send, share_recv, hop_send, hop_recv, *low,
):
    site = lax.axis_index("site")
    sec = lax.axis_index("sec")
    states, own, rows = ket.shape[:3]
    first = sec * own
    after = lax.rem(site + 1, sites)
    before = lax.rem(site + sites - 1, sites)

    def sibling(k):
        return lax.rem(sec + k, groups)

    def load_env(b):
        return pltpu.make_async_copy(env_hbm.at[b], env.at[b], env_sem.at[b])

    def load_ket(b):
        return pltpu.make_async_copy(ket_hbm.at[:, b], ket.at[:, b], ket_sem.at[b])

    def load_bra(b):
        return pltpu.make_async_copy(bra_hbm.at[:, b], bra.at[:, b], bra_sem.at[b])

    def share(t, k, b):
        return pltpu.make_async_remote_copy(
            src_ref=low[t].at[first + b],
            dst_ref=low[t].at[first + b],
            send_sem=share_send.at[t, k - 1, b],
            recv_sem=share_recv.at[t, k - 1, b],
            device_id=(site, sibling(k)),
            device_id_type=MESH,
        )

    def shared(t, k, b):
        row = lax.rem(sec + groups - k, groups) * own + b
        return pltpu.make_async_remote_copy(
            src_ref=low[t].at[row],
            dst_ref=low[t].at[row],
            send_sem=share_send.at[t, k - 1, b],
            recv_sem=share_recv.at[t, k - 1, b],
            device_id=(site, sibling(k)),
            device_id_type=MESH,
        )

    def hop(t, b, q):
        part = pl.ds(q * rows // PIECES, rows // PIECES)
        return pltpu.make_async_remote_copy(
            src_ref=staged.at[t, b, part],
            dst_ref=low[t + 1].at[first + b, part] if t < ITERS - 1 else out_ref.at[b, part],
            send_sem=hop_send.at[t, b, q],
            recv_sem=hop_recv.at[t, b, q],
            device_id=(after, sec),
            device_id_type=MESH,
        )

    def each(body):
        def one(b, carry):
            body(b)
            return carry

        lax.fori_loop(0, own, one, 0)

    barrier = pltpu.get_barrier_semaphore()
    for peer in [(after, sec), (before, sec)] + [(site, sibling(k)) for k in range(1, groups)]:
        pl.semaphore_signal(barrier, inc=1, device_id=peer, device_id_type=MESH)

    each(lambda b: load_env(b).start())
    each(lambda b: load_ket(b).start())
    each(lambda b: load_bra(b).start())
    pl.semaphore_wait(barrier, groups + 1)

    def open_own(b):
        load_env(b).wait()
        low[0][first + b] = env[b].astype(jnp.bfloat16)
        for k in range(1, groups):
            share(0, k, b).start()

    each(open_own)

    def advance(t, b):
        for p in range(states):
            if t == 0:
                bra_t[b, :, p * rows : (p + 1) * rows] = bra[p, b].T
            picked = low[t][source_ref[p, first + b]]
            half = jnp.dot(picked, ket[p, b], preferred_element_type=jnp.float32)
            halves[p * rows : (p + 1) * rows] = half.astype(jnp.bfloat16)
        for q in range(PIECES):
            part = pl.ds(q * rows // PIECES, rows // PIECES)
            total = jnp.dot(bra_t[b, part], halves[...], preferred_element_type=jnp.float32)
            staged[t, b, part] = total.astype(jnp.bfloat16)
            hop(t, b, q).start()

    for t in range(ITERS):
        if t > 0:

            def pass_on(b, t=t):
                for q in range(PIECES):
                    hop(t - 1, b, q).wait_recv()
                for k in range(1, groups):
                    share(t, k, b).start()

            each(pass_on)

        def arrive(b, t=t):
            for k in range(1, groups):
                shared(t, k, b).wait_recv()

        each(arrive)

        def work(b, t=t):
            if t == 0:
                load_ket(b).wait()
                load_bra(b).wait()
            advance(t, b)

        each(work)

    def finish(b):
        for t in range(ITERS):
            for q in range(PIECES):
                hop(t, b, q).wait_send()
            for k in range(1, groups):
                share(t, k, b).wait_send()
        for q in range(PIECES):
            hop(ITERS - 1, b, q).wait_recv()

    each(finish)


def body(sites, groups, env_in, ket, bra, source):
    _, states, own, rows, cols = ket.shape
    whole = own * groups
    low = jnp.bfloat16
    arrived = pl.pallas_call(
        functools.partial(kernel, sites, groups),
        out_shape=jax.ShapeDtypeStruct((own, rows, cols), low),
        in_specs=[pl.BlockSpec(memory_space=pltpu.SMEM)] + [pl.BlockSpec(memory_space=pl.ANY)] * 3,
        out_specs=pl.BlockSpec(memory_space=pl.ANY),
        scratch_shapes=[
            pltpu.VMEM((own, rows, cols), jnp.float32),
            pltpu.VMEM((states, own, rows, cols), low),
            pltpu.VMEM((states, own, rows, cols), low),
            pltpu.VMEM((own, cols, states * rows), low),
            pltpu.VMEM((states * rows, cols), low),
            pltpu.VMEM((ITERS, own, rows, cols), low),
            pltpu.SemaphoreType.DMA((own,)),
            pltpu.SemaphoreType.DMA((own,)),
            pltpu.SemaphoreType.DMA((own,)),
            pltpu.SemaphoreType.DMA((ITERS, groups - 1, own)),
            pltpu.SemaphoreType.DMA((ITERS, groups - 1, own)),
            pltpu.SemaphoreType.DMA((ITERS, own, PIECES)),
            pltpu.SemaphoreType.DMA((ITERS, own, PIECES)),
        ]
        + [pltpu.VMEM((whole, rows, cols), low)] * ITERS,
        compiler_params=pltpu.CompilerParams(collective_id=0, has_side_effects=True),
    )(source[0], env_in[0], ket[0], bra[0])
    return arrived.astype(jnp.float32)[None]


def solution(mesh):
    in_specs = (
        P("site", "sec", None, None),
        P("site", None, "sec", None, None),
        P("site", None, "sec", None, None),
        P("site", None, None),
    )
    out_specs = P("site", "sec", None, None)
    part = functools.partial(body, mesh.shape["site"], mesh.shape["sec"])
    return jax.shard_map(part, mesh=mesh, in_specs=in_specs, out_specs=out_specs, check_vma=False)
```
